1024 devices in a mesh: blk: 32 (over y_hi, z), narrow: 32 (over y_lo, x, core).
Axes of the slice: x: 8, y: 8 (y_hi: 4, y_lo: 2; y = y_hi * 2 + y_lo), z: 8, core: 2. Of those that a mesh axis runs over, the one named last changes fastest.
Arguments:
- factors_a: bfloat16 [2, 2048, 512], replicated, may hold values from -0.25 to 0.25
- factors_b: bfloat16 [512, 2048, 512], P('blk', 'narrow'), may hold values from -0.0078125 to 0.0078125
- amplitudes: bfloat16 [256, 2048, 2048], P('blk', 'narrow'), may hold values from -6 to 6
- screen: int32 [32, 16], replicated, may hold values from 0 to 1, as said below
Outputs:
- residual: float32 [3, 32, 256], P(None, 'blk', 'narrow')
The draws below stay inside these ranges and needn't reach their ends.
Inputs may be any that keep to these rules, and one draw needn't show every extreme that they name: `screen`: entry [i, s] is 1 where c sub-tile s is kept for pair tile i. Every row keeps 1 to 8 sub-tiles and some row keeps exactly 8.
All inputs are finite; a program needn't handle non-finite values.
Results may differ from the reference program's by a relative error of at most 0.0029.
Values may be sent and summed in bfloat16 or wider, within the bound.
A program may use at most 64 MiB of HBM per device.

```python
import jax
import jax.numpy as jnp
from jax import lax

V = 2048
NAUX = 512
CS = 128
AROWS = 2
BT = 16
P_SLAB = 8
STEPS = 3
PAIRS = 256
BW = 512
NSUB = 16
MOST = 8
N_BLK = 32


def draw_screen(key, part):
    key_count = jax.random.fold_in(key, 11)
    key_busy = jax.random.fold_in(key, 12)
    key_order = jax.random.fold_in(key, 13)
    counts = 1 + jax.random.randint(key_count, (N_BLK,), 0, 3)
    counts = jnp.minimum(counts, MOST)
    busiest = jax.random.randint(key_busy, (), 0, N_BLK)
    counts = jnp.where(jnp.arange(N_BLK) == busiest, MOST, counts)
    scores = jax.random.randint(key_order, (N_BLK, NSUB), 0, 1 << 20) * NSUB + jnp.arange(NSUB)[None, :]
    order = jnp.argsort(scores, axis=1)
    ranks = jnp.argsort(order, axis=1)
    return (ranks < counts[:, None]).astype(jnp.int32)


def levels(stream_key, extent, split, smallest, largest):
    def one(dim, parts):
        heights = jax.random.uniform(jax.random.fold_in(jax.random.fold_in(stream_key, 6), dim), (parts,), jnp.float32, smallest / len(split), largest / len(split))
        return jnp.repeat(jnp.exp(heights), extent[dim] // parts).reshape((-1,) + (1,) * (len(extent) - dim - 1))

    factor_of = one(*split[0])
    for cut in split[1:]:
        factor_of = factor_of * one(*cut)
    return factor_of


def normal_values(stream_key, dims, deviation, limit, pieces=(), kind=jnp.bfloat16):
    drawn = jax.random.normal(stream_key, dims, jnp.float32) * deviation
    if len(pieces) > 0:
        drawn = levels(stream_key, dims, pieces, -0.22, 0.18) * drawn
    return jnp.clip(drawn, min=-limit, max=limit).astype(kind)


def setup_inputs(seed: int = 0) -> dict:
    seeds = jax.random.split(jax.random.key(seed), 5)
    return {
        "factors_a": normal_values(seeds[0], (AROWS, V, NAUX), NAUX ** -0.5, 0.25),
        "factors_b": normal_values(seeds[1], (BW, V, NAUX), (2 * CS * V) ** -0.5, 0.0078125, ((0, 32), (1, 32))),
        "amplitudes": normal_values(seeds[2], (PAIRS, V, V), 1.0, 6.0, ((0, 32), (1, 32))),
        "screen": draw_screen(jax.random.fold_in(seeds[4], 71), 0),
    }


def reference(factors_a, factors_b, amplitudes, screen):
    tile_count = N_BLK

    def per_tile(tile_at):
        b_panel = lax.dynamic_slice_in_dim(factors_b, (tile_at * BT).astype(jnp.int32), BT, 0).reshape(BT * V, NAUX)
        slab_stack = jnp.stack([lax.dynamic_slice_in_dim(amplitudes, (((tile_at - offset) % tile_count) * P_SLAB).astype(jnp.int32), P_SLAB, 0) for offset in range(STEPS)])

        def add_tile(sub_at, running):
            sub_at = sub_at.astype(jnp.int32)

            def compute(running):
                factor_block = lax.dynamic_slice_in_dim(factors_a, sub_at * CS, CS, 1).reshape(AROWS * CS, NAUX)
                integral = jnp.dot(factor_block, b_panel.T, preferred_element_type=jnp.float32)
                integral = integral.astype(jnp.bfloat16).reshape(AROWS, CS, BT, V)
                amp_block = lax.dynamic_slice_in_dim(slab_stack, sub_at * CS, CS, 3)
                return running + jnp.einsum("xpdc,acbd->xpab", amp_block.astype(jnp.float32), integral.astype(jnp.float32))

            return lax.cond(screen[tile_at, sub_at] != 0, compute, lambda kept: kept, running)

        running = lax.fori_loop(0, V // CS, add_tile, jnp.zeros((STEPS, P_SLAB, AROWS, BT), jnp.float32))
        return running.reshape(STEPS, P_SLAB * AROWS * BT)

    results = lax.map(per_tile, jnp.arange(tile_count, dtype=jnp.int32))
    return jnp.transpose(results, (1, 0, 2))
```

```python
import functools

import jax
import jax.numpy as jnp
from jax import lax
from jax.experimental import pallas as pl
from jax.experimental.pallas import tpu as pltpu
from jax.sharding import PartitionSpec as P

MESH = pl.DeviceIdType.MESH
CS = 128
SLOTS = 8
STEPS = 3
DC = 16
NZ = 8
F32 = jnp.float32
BF16 = jnp.bfloat16


def kept_of(screen_ref, row, nsub):
    count = jnp.int32(0)
    at = [jnp.int32(0)] * SLOTS
    for sub in range(nsub):
        count = count + jnp.where(screen_ref[row, sub] != 0, 1, 0)
        at = [a + jnp.where(count <= slot, 1, 0) for slot, a in enumerate(at)]
    return [jnp.minimum(a, nsub - 1) for a in at], count


def kernel(
    n_blk, n_nar, f_hbm, b_hbm, a_hbm, screen_ref, out_ref,
    fv, bv, av, g, gr, br, ak0, ak1, fk0, fk1, integral, acc0, acc1, srow, rrow, fin,
    ld_sem, sb_sem, sa_sem, rb_sem, ra_sem, fwd_sem, rs_send, rs_recv, fin_sem,
):
    blk = lax.axis_index("blk")
    nar = lax.axis_index("narrow")
    n_a, n_virt, n_aux = f_hbm.shape
    n_b, n_d, _ = b_hbm.shape
    n_p = a_hbm.shape[0]
    chunks = n_d // DC
    nsub = n_virt // CS
    z = lax.rem(blk, NZ)
    up = lax.rem(blk + 1, n_blk)
    down = lax.rem(blk + n_blk - 1, n_blk)
    next_ring = lax.rem(blk + NZ, n_blk)
    last_ring = lax.rem(blk + n_blk - NZ, n_blk)
    is_top = lax.div(z + 1, NZ)
    is_low = 1 - lax.div(z + NZ - 1, NZ)

    load_b = pltpu.make_async_copy(b_hbm, bv, ld_sem.at[2])
    for sub in range(nsub):
        pltpu.make_async_copy(a_hbm.at[:, :, sub * CS : (sub + 1) * CS], av.at[sub], ld_sem.at[0]).start()
    for sub in range(nsub):
        pltpu.make_async_copy(f_hbm.at[:, sub * CS : (sub + 1) * CS, :], fv.at[sub], ld_sem.at[1]).start()
    load_b.start()

    barrier = pltpu.get_barrier_semaphore()

    @pl.loop(1, n_nar)
    def _(off):
        pl.semaphore_signal(barrier, inc=1, device_id=(blk, lax.rem(nar + off, n_nar)), device_id_type=MESH)

    for other in (up, down, next_ring, last_ring, blk - z + (NZ - 1 - z)):
        pl.semaphore_signal(barrier, inc=1, device_id=(other, nar), device_id_type=MESH)

    at0, n0 = kept_of(screen_ref, blk, nsub)
    at1, n1 = kept_of(screen_ref, up, nsub)
    at2, _ = kept_of(screen_ref, lax.rem(blk + 2, n_blk), nsub)
    pl.semaphore_wait(barrier, n_nar - 1 + 5)

    hb, hp = n_b // 2, n_p // 2

    def send_b(c, h):
        relay = is_low * h
        return pltpu.make_async_remote_copy(
            src_ref=b_hbm.at[pl.ds(h * hb, hb), pl.ds(c * DC, DC), :],
            dst_ref=br.at[relay, c, pl.ds(h * hb, hb)],
            send_sem=sb_sem,
            recv_sem=rb_sem.at[relay, c],
            device_id=(down * (1 - relay) + (blk + NZ - 1) * relay, nar),
            device_id_type=MESH,
        )

    def send_a(c, h):
        relay = is_top * h
        return pltpu.make_async_remote_copy(
            src_ref=g.at[c, pl.ds(h * hp, hp)],
            dst_ref=gr.at[relay, c, pl.ds(h * hp, hp)],
            send_sem=sa_sem,
            recv_sem=ra_sem.at[relay, c],
            device_id=(up * (1 - relay) + (blk + 1 - NZ) * relay, nar),
            device_id_type=MESH,
        )

    @pl.loop(0, chunks)
    def _(c):
        send_b(c, 1).start()
        send_b(c, 0).start()

    def keep_amps(dst, c, at):
        for slot in range(SLOTS):
            dst[c, :, :, slot * CS : (slot + 1) * CS] = av[at[slot], :, c * DC : (c + 1) * DC, :]

    pltpu.make_async_copy(av, av, ld_sem.at[0]).wait()
    for c in range(chunks):
        keep_amps(g, c, at2)
        send_a(c, 1).start()
        send_a(c, 0).start()

    def relay_on(c):
        @pl.when(z == 0)
        def _():
            here = gr.at[1, c, pl.ds(hp, hp)]
            pltpu.make_async_copy(here, here, ra_sem.at[1, c]).wait()
            pltpu.make_async_remote_copy(
                src_ref=here, dst_ref=gr.at[0, c, pl.ds(hp, hp)], send_sem=fwd_sem, recv_sem=ra_sem.at[0, c],
                device_id=(next_ring, nar), device_id_type=MESH,
            ).start()

        @pl.when(z == NZ - 1)
        def _():
            here = br.at[1, c, pl.ds(hb, hb)]
            pltpu.make_async_copy(here, here, rb_sem.at[1, c]).wait()
            pltpu.make_async_remote_copy(
                src_ref=here, dst_ref=br.at[0, c, pl.ds(hb, hb)], send_sem=fwd_sem, recv_sem=rb_sem.at[0, c],
                device_id=(last_ring, nar), device_id_type=MESH,
            ).start()

    for c in range(chunks):
        keep_amps(ak0, c, at0)
        keep_amps(ak1, c, at1)

    pltpu.make_async_copy(fv, fv, ld_sem.at[1]).wait()
    for fk, at, count in ((fk0, at0, n0), (fk1, at1, n1)):
        for slot in range(SLOTS):
            held = jnp.full((CS, n_aux), jnp.where(slot < count, 1.0, 0.0), F32).astype(BF16)
            for a in range(n_a):
                fk[a, slot * CS : (slot + 1) * CS, :] = fv[at[slot], a] * held
    load_b.wait()
    acc0[...] = jnp.zeros_like(acc0)
    acc1[...] = jnp.zeros_like(acc1)

    def add_chunk(fk, panel, amps, acc):
        for a in range(n_a):
            integral[...] = lax.dot_general(
                fk[a], panel, (((1,), (1,)), ((), ())), preferred_element_type=F32
            ).astype(BF16)
            tile = integral[...]
            for s, amp in enumerate(amps):
                acc[s, a] += jnp.dot(amp, tile, preferred_element_type=F32)

    rows_b, rows_p = n_b * DC, n_p * DC
    relay_on(0)

    @pl.loop(0, chunks)
    def _(c):
        panel = bv[:, pl.ds(pl.multiple_of(c * DC, DC), DC), :].reshape(rows_b, n_aux)
        add_chunk(fk0, panel, (ak0[c].reshape(rows_p, SLOTS * CS),), acc0)

    relay_on(1)

    @pl.loop(0, chunks)
    def _(c):
        @pl.when(c + 2 < chunks)
        def _():
            relay_on(c + 2)

        here = br.at[0, c]
        pltpu.make_async_copy(here, here, rb_sem.at[0, c]).wait()
        here = gr.at[0, c]
        pltpu.make_async_copy(here, here, ra_sem.at[0, c]).wait()
        panel = br[0, c].reshape(rows_b, n_aux)
        amps = (ak1[c].reshape(rows_p, SLOTS * CS), gr[0, c].reshape(rows_p, SLOTS * CS))
        add_chunk(fk1, panel, amps, acc1)

    same_d = lax.rem(lax.broadcasted_iota(jnp.int32, (rows_p, rows_b), 0), DC) == lax.rem(
        lax.broadcasted_iota(jnp.int32, (rows_p, rows_b), 1), DC
    )
    lane = lax.rem(lax.broadcasted_iota(jnp.int32, (n_p, 128), 1), DC)
    halves = rows_b // 128
    for a in range(n_a):
        sums = []
        for acc, s in ((acc0, 0), (acc1, 0), (acc1, 1)):
            kept = jnp.where(same_d, acc[s, a], 0.0)
            sums.append(kept.reshape(n_p, DC, rows_b).sum(axis=1))
        for half in range(halves):
            row = jnp.zeros((n_p, 128), F32)
            for s in range(STEPS):
                part = sums[s][:, half * 128 : (half + 1) * 128]
                for step in (8, 4, 2, 1):
                    part = part + pltpu.roll(part, 128 - step, 1)
                if s:
                    part = pltpu.roll(part, s, 1)
                row = jnp.where(lane == s, part, row)
            for q in range(n_p):
                srow[(q * n_a + a) * halves + half] = row[q : q + 1, :]

    def send_row(off):
        to = lax.rem(nar + off, n_nar)
        return pltpu.make_async_remote_copy(
            src_ref=srow.at[to], dst_ref=rrow.at[nar], send_sem=rs_send, recv_sem=rs_recv,
            device_id=(blk, to), device_id_type=MESH,
        )

    @pl.loop(1, n_nar)
    def _(off):
        send_row(off).start()

    rrow[nar] = srow[nar]
    others = rrow.at[pl.ds(0, n_nar - 1)]
    pltpu.make_async_copy(others, others, rs_recv).wait()
    total = rrow[...].sum(axis=0)
    fin[0] = total
    last = pltpu.make_async_remote_copy(
        src_ref=fin.at[0], dst_ref=fin.at[1], send_sem=fin_sem.at[0], recv_sem=fin_sem.at[1],
        device_id=(up, nar), device_id_type=MESH,
    )
    last.start()
    sent = srow.at[pl.ds(0, n_nar - 1)]
    pltpu.make_async_copy(sent, sent, rs_send).wait()
    pltpu.make_async_copy(g, g, sa_sem).wait()
    pltpu.make_async_copy(b_hbm, b_hbm, sb_sem).wait()

    @pl.when(z == 0)
    def _():
        here = gr.at[1, :, pl.ds(hp, hp)]
        pltpu.make_async_copy(here, here, fwd_sem).wait()

    @pl.when(z == NZ - 1)
    def _():
        here = br.at[1, :, pl.ds(hb, hb)]
        pltpu.make_async_copy(here, here, fwd_sem).wait()

    last.wait()
    out_ref[...] = fin[...]


def local(n_blk, n_nar, factors_a, factors_b, amplitudes, screen):
    n_a, n_virt, n_aux = factors_a.shape
    n_b, n_d, _ = factors_b.shape
    nsub = n_virt // CS
    n_p = amplitudes.shape[0]
    chunks = n_d // DC
    kept = SLOTS * CS
    any_spec = pl.BlockSpec(memory_space=pl.ANY)
    rows = pl.pallas_call(
        functools.partial(kernel, n_blk, n_nar),
        out_shape=jax.ShapeDtypeStruct((2, 1, 128), F32),
        in_specs=[any_spec, any_spec, any_spec, pl.BlockSpec(memory_space=pltpu.SMEM)],
        out_specs=pl.BlockSpec(memory_space=pltpu.VMEM),
        scratch_shapes=[
            pltpu.VMEM((nsub, n_a, CS, n_aux), BF16),
            pltpu.VMEM(factors_b.shape, BF16),
            pltpu.VMEM((nsub, n_p, n_d, CS), BF16),
            pltpu.VMEM((chunks, n_p, DC, kept), BF16),
            pltpu.VMEM((2, chunks, n_p, DC, kept), BF16),
            pltpu.VMEM((2, chunks, n_b, DC, n_aux), BF16),
            pltpu.VMEM((chunks, n_p, DC, kept), BF16),
            pltpu.VMEM((chunks, n_p, DC, kept), BF16),
            pltpu.VMEM((n_a, kept, n_aux), BF16),
            pltpu.VMEM((n_a, kept, n_aux), BF16),
            pltpu.VMEM((kept, n_b * DC), BF16),
            pltpu.VMEM((1, n_a, n_p * DC, n_b * DC), F32),
            pltpu.VMEM((2, n_a, n_p * DC, n_b * DC), F32),
            pltpu.VMEM((n_nar, 1, 128), F32),
            pltpu.VMEM((n_nar, 1, 128), F32),
            pltpu.VMEM((2, 1, 128), F32),
            pltpu.SemaphoreType.DMA((3,)),
            pltpu.SemaphoreType.DMA,
            pltpu.SemaphoreType.DMA,
            pltpu.SemaphoreType.DMA((2, chunks)),
            pltpu.SemaphoreType.DMA((2, chunks)),
            pltpu.SemaphoreType.DMA,
            pltpu.SemaphoreType.DMA,
            pltpu.SemaphoreType.DMA,
            pltpu.SemaphoreType.DMA((2,)),
        ],
        compiler_params=pltpu.CompilerParams(collective_id=0, has_side_effects=True),
        name="ladder",
    )(factors_a, factors_b, amplitudes, screen)
    from_row = jnp.concatenate([rows[:1], rows[1:], rows[1:]], 0)
    step = lax.broadcasted_iota(jnp.int32, (STEPS, 8, 128), 0)
    index = lax.broadcasted_iota(jnp.int32, (STEPS, 8, 128), 1)
    lane = lax.broadcasted_iota(jnp.int32, (STEPS, 8, 128), 2)
    picked = jnp.where(lane == index * DC + step, from_row, 0.0)
    return picked.sum(axis=2).reshape(STEPS, 1, 8)


def solution(mesh):
    return jax.shard_map(
        functools.partial(local, mesh.shape["blk"], mesh.shape["narrow"]),
        mesh=mesh,
        in_specs=(P(), P("blk", "narrow", None), P("blk", "narrow", None), P()),
        out_specs=P(None, "blk", "narrow"),
        check_vma=False,
    )
```

```python
import functools

import jax
import jax.numpy as jnp
from jax import lax
from jax.experimental import pallas as pl
from jax.experimental.pallas import tpu as pltpu
from jax.sharding import PartitionSpec as P

MESH = pl.DeviceIdType.MESH
CS = 128
SLOTS = 8
STEPS = 3
DC = 16
PIECES = 2
RELAYED = 7
NZ = 8
F32 = jnp.float32
BF16 = jnp.bfloat16


def kept_of(screen_ref, row, nsub):
    count = jnp.int32(0)
    at = [jnp.int32(0)] * SLOTS
    for sub in range(nsub):
        count = count + jnp.where(screen_ref[sub, row] != 0, 1, 0)
        at = [a + jnp.where(count <= slot, 1, 0) for slot, a in enumerate(at)]
    return [jnp.minimum(a, nsub - 1) for a in at], count


def kernel(
    n_blk, n_nar, f_hbm, b_hbm, a_hbm, screen_hbm, out_ref,
    screen_ref, fv, bv, av, g, gr, br, ak0, ak1, fk0, fk1, integral, acc0, acc1, srow, rrow, fin,
    ld_sem, sb_sem, sa_sem, rb_sem, ra_sem, fwd_sem, rs_send, rs_recv,
):
    blk = lax.axis_index("blk")
    nar = lax.axis_index("narrow")
    n_a, n_virt, n_aux = f_hbm.shape
    n_b, n_d, _ = b_hbm.shape
    n_p = a_hbm.shape[0]
    chunks = n_d // DC
    nsub = n_virt // CS
    z = lax.rem(blk, NZ)
    up = lax.rem(blk + 1, n_blk)
    down = lax.rem(blk + n_blk - 1, n_blk)
    next_ring = lax.rem(blk + NZ, n_blk)
    last_ring = lax.rem(blk + n_blk - NZ, n_blk)
    is_top = lax.div(z + 1, NZ)
    is_low = 1 - lax.div(z + NZ - 1, NZ)

    barrier = pltpu.get_barrier_semaphore()

    for other in (up, down, next_ring, last_ring, blk - z + (NZ - 1 - z)):
        pl.semaphore_signal(barrier, inc=1, device_id=(other, nar), device_id_type=MESH)

    @pl.loop(1, n_nar)
    def _(off):
        pl.semaphore_signal(barrier, inc=1, device_id=(blk, lax.rem(nar + off, n_nar)), device_id_type=MESH)
        pl.semaphore_signal(barrier, inc=1, device_id=(down, lax.rem(nar + off, n_nar)), device_id_type=MESH)

    load_s = pltpu.make_async_copy(screen_hbm, screen_ref, ld_sem.at[3])
    load_s.start()
    for c in range(chunks):
        pltpu.make_async_copy(b_hbm.at[:, c * DC : (c + 1) * DC, :], bv.at[c], ld_sem.at[2]).start()
    for sub in range(nsub):
        pltpu.make_async_copy(a_hbm.at[:, :, sub * CS : (sub + 1) * CS], av.at[sub], ld_sem.at[0]).start()
    for sub in range(nsub):
        pltpu.make_async_copy(f_hbm.at[:, sub * CS : (sub + 1) * CS, :], fv.at[sub], ld_sem.at[1]).start()
    load_s.wait()
    at0, n0 = kept_of(screen_ref, blk, nsub)
    at1, n1 = kept_of(screen_ref, up, nsub)
    at2, _ = kept_of(screen_ref, lax.rem(blk + 2, n_blk), nsub)

    def keep_amps(dst, c, at):
        for slot in range(SLOTS):
            dst[c, :, :, slot * CS : (slot + 1) * CS] = av[at[slot], :, c * DC : (c + 1) * DC, :]

    pltpu.make_async_copy(av, av, ld_sem.at[0]).wait()
    for c in range(chunks):
        keep_amps(g, c, at2)
    pltpu.make_async_copy(bv, bv, ld_sem.at[2]).wait()
    pl.semaphore_wait(barrier, 2 * (n_nar - 1) + 5)

    hb, hp = n_b // 2, n_p // 2
    qb, qp = hb // PIECES, hp // PIECES

    def send_b(c, first, size, relay, piece):
        return pltpu.make_async_remote_copy(
            src_ref=bv.at[c, pl.ds(first, size)],
            dst_ref=br.at[relay, c, pl.ds(first, size)],
            send_sem=sb_sem,
            recv_sem=rb_sem.at[(c * 2 + first // hb) * (1 - relay) + (chunks * 2 + piece) * relay],
            device_id=(down * (1 - relay) + (blk + NZ - 1) * relay, nar),
            device_id_type=MESH,
        )

    def send_a(c, first, size, relay, piece):
        return pltpu.make_async_remote_copy(
            src_ref=g.at[c, pl.ds(first, size)],
            dst_ref=gr.at[relay, c, pl.ds(first, size)],
            send_sem=sa_sem,
            recv_sem=ra_sem.at[c * (1 - relay) + (chunks + piece) * relay],
            device_id=(up * (1 - relay) + (blk + 1 - NZ) * relay, nar),
            device_id_type=MESH,
        )

    def panels_down():
        @pl.loop(0, chunks)
        def _(c):
            for u in range(PIECES):
                piece = c * PIECES + u
                send_b(c, hb + u * qb, qb, is_low * (1 - lax.div(piece, RELAYED)), piece).start()
            send_b(c, 0, hb, 0, 0).start()

    def amps_up():
        @pl.loop(0, chunks)
        def _(c):
            for u in range(PIECES):
                piece = c * PIECES + u
                send_a(c, hp + u * qp, qp, is_top * (1 - lax.div(piece, RELAYED)), piece).start()
            send_a(c, 0, hp, 0, 0).start()

    @pl.when(z < NZ - 1)
    def _():
        panels_down()
        amps_up()

    @pl.when(z == NZ - 1)
    def _():
        amps_up()
        panels_down()

    def relay_on(piece):
        c, u = lax.div(piece, PIECES), lax.rem(piece, PIECES)

        @pl.when(z == 0)
        def _():
            part = pl.ds(hp + u * qp, qp)
            here = gr.at[1, c, part]
            pltpu.make_async_copy(here, here, ra_sem.at[chunks + piece]).wait()
            pltpu.make_async_remote_copy(
                src_ref=here, dst_ref=gr.at[0, c, part], send_sem=fwd_sem.at[piece], recv_sem=ra_sem.at[c],
                device_id=(next_ring, nar), device_id_type=MESH,
            ).start()

        @pl.when(z == NZ - 1)
        def _():
            part = pl.ds(hb + u * qb, qb)
            here = br.at[1, c, part]
            pltpu.make_async_copy(here, here, rb_sem.at[chunks * 2 + piece]).wait()
            pltpu.make_async_remote_copy(
                src_ref=here, dst_ref=br.at[0, c, part], send_sem=fwd_sem.at[piece], recv_sem=rb_sem.at[c * 2 + 1],
                device_id=(last_ring, nar), device_id_type=MESH,
            ).start()

    for c in range(chunks):
        keep_amps(ak0, c, at0)
        keep_amps(ak1, c, at1)

    pltpu.make_async_copy(fv, fv, ld_sem.at[1]).wait()
    for fk, at, count in ((fk0, at0, n0), (fk1, at1, n1)):
        for slot in range(SLOTS):
            held = jnp.full((CS, n_aux), jnp.where(slot < count, 1.0, 0.0), F32).astype(BF16)
            for a in range(n_a):
                fk[a, slot * CS : (slot + 1) * CS, :] = fv[at[slot], a] * held
    acc0[...] = jnp.zeros_like(acc0)
    acc1[...] = jnp.zeros_like(acc1)

    def integrals(fk, panel, half):
        cols = slice(half * hb * DC, (half + 1) * hb * DC)
        for a in range(n_a):
            integral[a, :, cols] = lax.dot_general(
                fk[a], panel.reshape(hb * DC, n_aux), (((1,), (1,)), ((), ())), preferred_element_type=F32
            ).astype(BF16)

    def add_amps(amps, acc):
        for a in range(n_a):
            tile = integral[a]
            for s, amp in enumerate(amps):
                acc[s, a] += jnp.dot(amp, tile, preferred_element_type=F32)

    rows_b, rows_p = n_b * DC, n_p * DC
    relay_on(0)

    @pl.loop(0, chunks)
    def _(c):
        for half in range(2):
            integrals(fk0, bv[c, half * hb : (half + 1) * hb], half)
        add_amps((ak0[c].reshape(rows_p, SLOTS * CS),), acc0)
        relay_on(c + 1)

    same_d = lax.rem(lax.broadcasted_iota(jnp.int32, (rows_p, rows_b), 0), DC) == lax.rem(
        lax.broadcasted_iota(jnp.int32, (rows_p, rows_b), 1), DC
    )
    lane_s = lax.rem(lax.broadcasted_iota(jnp.int32, (n_p, 128), 1), DC)
    halves = rows_b // 128

    def write_rows(terms, to):
        for a in range(n_a):
            sums = []
            for acc, at, _ in terms:
                kept = jnp.where(same_d, acc[at, a], 0.0)
                sums.append(kept.reshape(n_p, DC, rows_b).sum(axis=1))
            for half in range(halves):
                row = jnp.zeros((n_p, 128), F32)
                for part, (_, _, s) in zip(sums, terms):
                    part = part[:, half * 128 : (half + 1) * 128]
                    for step in (8, 4, 2, 1):
                        part = part + pltpu.roll(part, 128 - step, 1)
                    if s:
                        part = pltpu.roll(part, s, 1)
                    row = jnp.where(lane_s == s, part, row)
                for q in range(n_p):
                    srow[to, (q * n_a + a) * halves + half] = row[q : q + 1, :]

    def send_row(which, tile, off):
        to = lax.rem(nar + off, n_nar)
        return pltpu.make_async_remote_copy(
            src_ref=srow.at[which, to], dst_ref=rrow.at[which, nar], send_sem=rs_send.at[which], recv_sem=rs_recv.at[which],
            device_id=(tile, to), device_id_type=MESH,
        )

    write_rows(((acc0, 0, 0),), 0)

    @pl.loop(1, n_nar)
    def _(off):
        send_row(0, blk, off).start()

    rrow[0, nar] = srow[0, nar]

    @pl.loop(0, chunks)
    def _(c):
        @pl.when(c + chunks + 1 < RELAYED)
        def _():
            relay_on(c + chunks + 1)

        for half in (1, 0):
            here = br.at[0, c, pl.ds(half * hb, hb)]
            pltpu.make_async_copy(here, here, rb_sem.at[c * 2 + half]).wait()
            integrals(fk1, br[0, c, half * hb : (half + 1) * hb], half)
        here = gr.at[0, c]
        pltpu.make_async_copy(here, here, ra_sem.at[c]).wait()
        add_amps((ak1[c].reshape(rows_p, SLOTS * CS), gr[0, c].reshape(rows_p, SLOTS * CS)), acc1)

    write_rows(((acc1, 0, 1), (acc1, 1, 2)), 1)

    @pl.loop(0, n_nar)
    def _(off):
        send_row(1, up, off).start()

    here = rrow.at[0, pl.ds(0, n_nar - 1)]
    pltpu.make_async_copy(here, here, rs_recv.at[0]).wait()
    fin[0] = rrow[0].sum(axis=0)
    pltpu.make_async_copy(rrow.at[1], rrow.at[1], rs_recv.at[1]).wait()
    fin[1] = rrow[1].sum(axis=0)
    sent = srow.at[0, pl.ds(0, n_nar - 1)]
    pltpu.make_async_copy(sent, sent, rs_send.at[0]).wait()
    pltpu.make_async_copy(srow.at[1], srow.at[1], rs_send.at[1]).wait()
    pltpu.make_async_copy(g, g, sa_sem).wait()
    pltpu.make_async_copy(bv, bv, sb_sem).wait()

    @pl.loop(0, RELAYED)
    def _(piece):
        @pl.when(z == 0)
        def _():
            here = gr.at[1, 0, pl.ds(hp, qp)]
            pltpu.make_async_copy(here, here, fwd_sem.at[piece]).wait()

        @pl.when(z == NZ - 1)
        def _():
            here = br.at[1, 0, pl.ds(hb, qb)]
            pltpu.make_async_copy(here, here, fwd_sem.at[piece]).wait()

    step = lax.broadcasted_iota(jnp.int32, (8, 128), 0)
    lane = lax.broadcasted_iota(jnp.int32, (8, 128), 1)
    held = jnp.where(step == 0, fin[0], fin[1])
    spread = jnp.take_along_axis(held, lax.rem(lane * DC + step, 128), axis=1)
    for s in range(STEPS):
        out_ref[s] = spread[s : s + 1, : out_ref.shape[2]]


def local(n_blk, n_nar, factors_a, factors_b, amplitudes, screen):
    n_a, n_virt, n_aux = factors_a.shape
    n_b, n_d, _ = factors_b.shape
    nsub = n_virt // CS
    n_p = amplitudes.shape[0]
    chunks = n_d // DC
    kept = SLOTS * CS
    any_spec = pl.BlockSpec(memory_space=pl.ANY)
    return pl.pallas_call(
        functools.partial(kernel, n_blk, n_nar),
        out_shape=jax.ShapeDtypeStruct((STEPS, 1, n_a * n_b * n_p // n_nar), F32),
        in_specs=[any_spec] * 4,
        out_specs=pl.BlockSpec(memory_space=pltpu.VMEM),
        scratch_shapes=[
            pltpu.SMEM(screen.shape[::-1], jnp.int32),
            pltpu.VMEM((nsub, n_a, CS, n_aux), BF16),
            pltpu.VMEM((chunks, n_b, DC, n_aux), BF16),
            pltpu.VMEM((nsub, n_p, n_d, CS), BF16),
            pltpu.VMEM((chunks, n_p, DC, kept), BF16),
            pltpu.VMEM((2, chunks, n_p, DC, kept), BF16),
            pltpu.VMEM((2, chunks, n_b, DC, n_aux), BF16),
            pltpu.VMEM((chunks, n_p, DC, kept), BF16),
            pltpu.VMEM((chunks, n_p, DC, kept), BF16),
            pltpu.VMEM((n_a, kept, n_aux), BF16),
            pltpu.VMEM((n_a, kept, n_aux), BF16),
            pltpu.VMEM((n_a, kept, n_b * DC), BF16),
            pltpu.VMEM((1, n_a, n_p * DC, n_b * DC), F32),
            pltpu.VMEM((2, n_a, n_p * DC, n_b * DC), F32),
            pltpu.VMEM((2, n_nar, 1, 128), F32),
            pltpu.VMEM((2, n_nar, 1, 128), F32),
            pltpu.VMEM((2, 1, 128), F32),
            pltpu.SemaphoreType.DMA((4,)),
            pltpu.SemaphoreType.DMA,
            pltpu.SemaphoreType.DMA,
            pltpu.SemaphoreType.DMA((chunks * (2 + PIECES),)),
            pltpu.SemaphoreType.DMA((chunks * (1 + PIECES),)),
            pltpu.SemaphoreType.DMA((RELAYED,)),
            pltpu.SemaphoreType.DMA((2,)),
            pltpu.SemaphoreType.DMA((2,)),
        ],
        compiler_params=pltpu.CompilerParams(collective_id=0, has_side_effects=True),
        name="ladder",
    )(factors_a, factors_b, amplitudes, screen.T)


def solution(mesh):
    return jax.shard_map(
        functools.partial(local, mesh.shape["blk"], mesh.shape["narrow"]),
        mesh=mesh,
        in_specs=(P(), P("blk", "narrow", None), P("blk", "narrow", None), P()),
        out_specs=P(None, "blk", "narrow"),
        check_vma=False,
    )
```

```python
import functools

import jax
import jax.numpy as jnp
from jax import lax
from jax.experimental import pallas as pl
from jax.experimental.pallas import tpu as pltpu
from jax.sharding import PartitionSpec as P

MESH = pl.DeviceIdType.MESH
CS = 128
SLOTS = 8
STEPS = 3
DC = 16
PIECES = 2
PER = PIECES // 2 or 1
RELAYED = 7
NZ = 8
F32 = jnp.float32
BF16 = jnp.bfloat16


def kept_of(screen_ref, row, nsub):
    count = jnp.int32(0)
    at = [jnp.int32(0)] * SLOTS
    for sub in range(nsub):
        count = count + jnp.where(screen_ref[sub, row] != 0, 1, 0)
        at = [a + jnp.where(count <= slot, 1, 0) for slot, a in enumerate(at)]
    return [jnp.minimum(a, nsub - 1) for a in at], count


def kernel(
    n_blk, n_nar, f_hbm, b_hbm, a_hbm, screen_hbm, out_ref,
    screen_ref, fv, bv, av, g, gr, br, ak0, ak1, fk0, fk1, integral, acc0, acc1, srow, rrow, fin,
    ld_sem, sb_sem, sa_sem, rb_sem, ra_sem, fwd_sem, rs_send, rs_recv,
):
    blk = lax.axis_index("blk")
    nar = lax.axis_index("narrow")
    n_a, n_virt, n_aux = f_hbm.shape
    n_b, n_d, _ = b_hbm.shape
    n_p = a_hbm.shape[0]
    chunks = n_d // DC
    nsub = n_virt // CS
    z = lax.rem(blk, NZ)
    up = lax.rem(blk + 1, n_blk)
    down = lax.rem(blk + n_blk - 1, n_blk)
    next_ring = lax.rem(blk + NZ, n_blk)
    last_ring = lax.rem(blk + n_blk - NZ, n_blk)
    is_top = lax.div(z + 1, NZ)
    is_low = 1 - lax.div(z + NZ - 1, NZ)

    barrier = pltpu.get_barrier_semaphore()

    for other in (up, down, next_ring, last_ring, blk - z + (NZ - 1 - z)):
        pl.semaphore_signal(barrier, inc=1, device_id=(other, nar), device_id_type=MESH)

    @pl.loop(1, n_nar)
    def _(off):
        pl.semaphore_signal(barrier, inc=1, device_id=(blk, lax.rem(nar + off, n_nar)), device_id_type=MESH)
        pl.semaphore_signal(barrier, inc=1, device_id=(down, lax.rem(nar + off, n_nar)), device_id_type=MESH)

    load_s = pltpu.make_async_copy(screen_hbm, screen_ref, ld_sem.at[3])
    load_s.start()
    for sub in range(nsub):
        pltpu.make_async_copy(a_hbm.at[:, :, sub * CS : (sub + 1) * CS], av.at[sub], ld_sem.at[0]).start()
    for c in range(chunks):
        pltpu.make_async_copy(b_hbm.at[:, c * DC : (c + 1) * DC, :], bv.at[c], ld_sem.at[2]).start()
    for sub in range(nsub):
        pltpu.make_async_copy(f_hbm.at[:, sub * CS : (sub + 1) * CS, :], fv.at[sub], ld_sem.at[1]).start()
    load_s.wait()
    at0, n0 = kept_of(screen_ref, blk, nsub)
    at1, n1 = kept_of(screen_ref, up, nsub)
    at2, _ = kept_of(screen_ref, lax.rem(blk + 2, n_blk), nsub)

    def keep_amps(dst, c, at):
        for slot in range(SLOTS):
            dst[c, :, :, slot * CS : (slot + 1) * CS] = av[at[slot], :, c * DC : (c + 1) * DC, :]

    pltpu.make_async_copy(av, av, ld_sem.at[0]).wait()
    for c in range(chunks):
        keep_amps(g, c, at2)
    pltpu.make_async_copy(bv, bv, ld_sem.at[2]).wait()
    pl.semaphore_wait(barrier, 2 * (n_nar - 1) + 5)

    hb, hp = n_b // 2, n_p // 2
    qb, qp = hb // PIECES, hp // PIECES

    def send_b(c, first, size, relay, piece):
        return pltpu.make_async_remote_copy(
            src_ref=bv.at[c, pl.ds(first, size)],
            dst_ref=br.at[relay, c, pl.ds(first, size)],
            send_sem=sb_sem,
            recv_sem=rb_sem.at[(c * 2 + first // hb) * (1 - relay) + (chunks * 2 + piece) * relay],
            device_id=(down * (1 - relay) + (blk + NZ - 1) * relay, nar),
            device_id_type=MESH,
        )

    def send_a(c, first, size, relay, piece):
        return pltpu.make_async_remote_copy(
            src_ref=g.at[c, pl.ds(first, size)],
            dst_ref=gr.at[relay, c, pl.ds(first, size)],
            send_sem=sa_sem,
            recv_sem=ra_sem.at[c * (1 - relay) + (chunks + piece) * relay],
            device_id=(up * (1 - relay) + (blk + 1 - NZ) * relay, nar),
            device_id_type=MESH,
        )

    def panels_down():
        @pl.loop(0, chunks)
        def _(c):
            for u in range(PIECES):
                piece = c * PIECES + u
                send_b(c, hb + u * qb, qb, is_low * (1 - lax.div(piece, RELAYED)), piece).start()
            send_b(c, 0, hb, 0, 0).start()

    def amps_up():
        @pl.loop(0, chunks)
        def _(c):
            for u in range(PIECES):
                piece = c * PIECES + u
                send_a(c, hp + u * qp, qp, is_top * (1 - lax.div(piece, RELAYED)), piece).start()
            send_a(c, 0, hp, 0, 0).start()

    @pl.when(z < NZ - 1)
    def _():
        panels_down()
        amps_up()

    @pl.when(z == NZ - 1)
    def _():
        amps_up()
        panels_down()

    def relay_on(piece):
        c, u = lax.div(piece, PIECES), lax.rem(piece, PIECES)

        @pl.when(z == 0)
        def _():
            part = pl.ds(hp + u * qp, qp)
            here = gr.at[1, c, part]
            pltpu.make_async_copy(here, here, ra_sem.at[chunks + piece]).wait()
            pltpu.make_async_remote_copy(
                src_ref=here, dst_ref=gr.at[0, c, part], send_sem=fwd_sem.at[piece], recv_sem=ra_sem.at[c],
                device_id=(next_ring, nar), device_id_type=MESH,
            ).start()

        @pl.when(z == NZ - 1)
        def _():
            part = pl.ds(hb + u * qb, qb)
            here = br.at[1, c, part]
            pltpu.make_async_copy(here, here, rb_sem.at[chunks * 2 + piece]).wait()
            pltpu.make_async_remote_copy(
                src_ref=here, dst_ref=br.at[0, c, part], send_sem=fwd_sem.at[piece], recv_sem=rb_sem.at[c * 2 + 1],
                device_id=(last_ring, nar), device_id_type=MESH,
            ).start()

    for c in range(chunks):
        keep_amps(ak0, c, at0)
        keep_amps(ak1, c, at1)

    pltpu.make_async_copy(fv, fv, ld_sem.at[1]).wait()
    for fk, at, count in ((fk0, at0, n0), (fk1, at1, n1)):
        for slot in range(SLOTS):
            held = jnp.full((CS, n_aux), jnp.where(slot < count, 1.0, 0.0), F32).astype(BF16)
            for a in range(n_a):
                fk[a, slot * CS : (slot + 1) * CS, :] = fv[at[slot], a] * held
    acc0[...] = jnp.zeros_like(acc0)
    acc1[...] = jnp.zeros_like(acc1)

    def integrals(fk, panel):
        for a in range(n_a):
            integral[a] = lax.dot_general(
                fk[a], panel.reshape(n_b * DC, n_aux), (((1,), (1,)), ((), ())), preferred_element_type=F32
            ).astype(BF16)

    def add_amps(amps, acc):
        for a in range(n_a):
            tile = integral[a]
            for s, amp in enumerate(amps):
                acc[s, a] += jnp.dot(amp, tile, preferred_element_type=F32)

    rows_b, rows_p = n_b * DC, n_p * DC
    def relay_step(step):
        for u in range(PER):
            piece = step * PER + u

            @pl.when(piece < RELAYED)
            def _(piece=piece):
                relay_on(piece)

    relay_step(jnp.int32(0))

    @pl.loop(0, chunks)
    def _(c):
        integrals(fk0, bv[c])
        add_amps((ak0[c].reshape(rows_p, SLOTS * CS),), acc0)
        relay_step(c + 1)

    same_d = lax.rem(lax.broadcasted_iota(jnp.int32, (rows_p, rows_b), 0), DC) == lax.rem(
        lax.broadcasted_iota(jnp.int32, (rows_p, rows_b), 1), DC
    )
    lane_s = lax.rem(lax.broadcasted_iota(jnp.int32, (n_p, 128), 1), DC)
    halves = rows_b // 128

    def write_rows(terms, to):
        for a in range(n_a):
            sums = []
            for acc, at, _ in terms:
                kept = jnp.where(same_d, acc[at, a], 0.0)
                sums.append(kept.reshape(n_p, DC, rows_b).sum(axis=1))
            for half in range(halves):
                row = jnp.zeros((n_p, 128), F32)
                for part, (_, _, s) in zip(sums, terms):
                    part = part[:, half * 128 : (half + 1) * 128]
                    for step in (8, 4, 2, 1):
                        part = part + pltpu.roll(part, 128 - step, 1)
                    if s:
                        part = pltpu.roll(part, s, 1)
                    row = jnp.where(lane_s == s, part, row)
                for q in range(n_p):
                    srow[to, (q * n_a + a) * halves + half] = row[q : q + 1, :]

    def send_row(which, tile, off):
        to = lax.rem(nar + off, n_nar)
        return pltpu.make_async_remote_copy(
            src_ref=srow.at[which, to], dst_ref=rrow.at[which, nar], send_sem=rs_send.at[which], recv_sem=rs_recv.at[which],
            device_id=(tile, to), device_id_type=MESH,
        )

    write_rows(((acc0, 0, 0),), 0)

    @pl.loop(1, n_nar)
    def _(off):
        send_row(0, blk, off).start()

    rrow[0, nar] = srow[0, nar]

    @pl.loop(0, chunks)
    def _(c):
        relay_step(c + chunks + 1)

        for half in (1, 0):
            here = br.at[0, c, pl.ds(half * hb, hb)]
            pltpu.make_async_copy(here, here, rb_sem.at[c * 2 + half]).wait()
        integrals(fk1, br[0, c])
        here = gr.at[0, c]
        pltpu.make_async_copy(here, here, ra_sem.at[c]).wait()
        add_amps((ak1[c].reshape(rows_p, SLOTS * CS), gr[0, c].reshape(rows_p, SLOTS * CS)), acc1)

    write_rows(((acc1, 0, 1), (acc1, 1, 2)), 1)

    @pl.loop(0, n_nar)
    def _(off):
        send_row(1, up, off).start()

    here = rrow.at[0, pl.ds(0, n_nar - 1)]
    pltpu.make_async_copy(here, here, rs_recv.at[0]).wait()
    fin[0] = rrow[0].sum(axis=0)
    pltpu.make_async_copy(rrow.at[1], rrow.at[1], rs_recv.at[1]).wait()
    fin[1] = rrow[1].sum(axis=0)
    sent = srow.at[0, pl.ds(0, n_nar - 1)]
    pltpu.make_async_copy(sent, sent, rs_send.at[0]).wait()
    pltpu.make_async_copy(srow.at[1], srow.at[1], rs_send.at[1]).wait()
    pltpu.make_async_copy(g, g, sa_sem).wait()
    pltpu.make_async_copy(bv, bv, sb_sem).wait()

    @pl.loop(0, RELAYED)
    def _(piece):
        @pl.when(z == 0)
        def _():
            here = gr.at[1, 0, pl.ds(hp, qp)]
            pltpu.make_async_copy(here, here, fwd_sem.at[piece]).wait()

        @pl.when(z == NZ - 1)
        def _():
            here = br.at[1, 0, pl.ds(hb, qb)]
            pltpu.make_async_copy(here, here, fwd_sem.at[piece]).wait()

    step = lax.broadcasted_iota(jnp.int32, (8, 128), 0)
    lane = lax.broadcasted_iota(jnp.int32, (8, 128), 1)
    held = jnp.where(step == 0, fin[0], fin[1])
    spread = jnp.take_along_axis(held, lax.rem(lane * DC + step, 128), axis=1)
    for s in range(STEPS):
        out_ref[s] = spread[s : s + 1, : out_ref.shape[2]]


def local(n_blk, n_nar, factors_a, factors_b, amplitudes, screen):
    n_a, n_virt, n_aux = factors_a.shape
    n_b, n_d, _ = factors_b.shape
    nsub = n_virt // CS
    n_p = amplitudes.shape[0]
    chunks = n_d // DC
    kept = SLOTS * CS
    any_spec = pl.BlockSpec(memory_space=pl.ANY)
    return pl.pallas_call(
        functools.partial(kernel, n_blk, n_nar),
        out_shape=jax.ShapeDtypeStruct((STEPS, 1, n_a * n_b * n_p // n_nar), F32),
        in_specs=[any_spec] * 4,
        out_specs=pl.BlockSpec(memory_space=pltpu.VMEM),
        scratch_shapes=[
            pltpu.SMEM(screen.shape[::-1], jnp.int32),
            pltpu.VMEM((nsub, n_a, CS, n_aux), BF16),
            pltpu.VMEM((chunks, n_b, DC, n_aux), BF16),
            pltpu.VMEM((nsub, n_p, n_d, CS), BF16),
            pltpu.VMEM((chunks, n_p, DC, kept), BF16),
            pltpu.VMEM((2, chunks, n_p, DC, kept), BF16),
            pltpu.VMEM((2, chunks, n_b, DC, n_aux), BF16),
            pltpu.VMEM((chunks, n_p, DC, kept), BF16),
            pltpu.VMEM((chunks, n_p, DC, kept), BF16),
            pltpu.VMEM((n_a, kept, n_aux), BF16),
            pltpu.VMEM((n_a, kept, n_aux), BF16),
            pltpu.VMEM((n_a, kept, n_b * DC), BF16),
            pltpu.VMEM((1, n_a, n_p * DC, n_b * DC), F32),
            pltpu.VMEM((2, n_a, n_p * DC, n_b * DC), F32),
            pltpu.VMEM((2, n_nar, 1, 128), F32),
            pltpu.VMEM((2, n_nar, 1, 128), F32),
            pltpu.VMEM((2, 1, 128), F32),
            pltpu.SemaphoreType.DMA((4,)),
            pltpu.SemaphoreType.DMA,
            pltpu.SemaphoreType.DMA,
            pltpu.SemaphoreType.DMA((chunks * (2 + PIECES),)),
            pltpu.SemaphoreType.DMA((chunks * (1 + PIECES),)),
            pltpu.SemaphoreType.DMA((RELAYED,)),
            pltpu.SemaphoreType.DMA((2,)),
            pltpu.SemaphoreType.DMA((2,)),
        ],
        compiler_params=pltpu.CompilerParams(collective_id=0, has_side_effects=True),
        name="ladder",
    )(factors_a, factors_b, amplitudes, screen.T)


def solution(mesh):
    return jax.shard_map(
        functools.partial(local, mesh.shape["blk"], mesh.shape["narrow"]),
        mesh=mesh,
        in_specs=(P(), P("blk", "narrow", None), P("blk", "narrow", None), P()),
        out_specs=P(None, "blk", "narrow"),
        check_vma=False,
    )
```
